32 devices in a mesh: runs: 2 (over y), tiles: 16 (over z, x, core).
Axes of the slice: x: 2, y: 2, z: 4, core: 2. Of those that a mesh axis runs over, the one named last changes fastest.
Arguments:
- features: bfloat16 [32, 256, 2048], P(('runs', 'tiles')), parts along dimension 0, may hold values from -6 to 6
- conv_weight: bfloat16 [2, 2, 9, 256, 256], replicated, may hold values from -0.125 to 0.125
- proj_weight: bfloat16 [2, 256, 128], replicated, may hold values from -0.375 to 0.375
- back_weight: bfloat16 [2, 128, 256], replicated, may hold values from -0.5 to 0.5
- sea_fraction: float32 [16, 2048], P('tiles'), may hold values from 0 to 1
- halo_source: int32 [16, 2, 128], P('tiles'), may hold values from 0 to 256, as said below
- src_cells: int32 [16, 5, 4, 128], P('tiles'), may hold values from 0 to 2047
- dst_cells: int32 [16, 5, 4, 128], P('tiles'), may hold values from 0 to 2048, as said below
Outputs:
- updated: bfloat16 [32, 256, 2048], P(('runs', 'tiles')), parts along dimension 0
The draws below stay inside these ranges and needn't reach their ends.
There are 2 independent parts, one for each index of `runs`. The reference program is written for one: setup_inputs(seed, part) draws one part's arguments, and reference() takes and returns one part's arrays. A program takes and returns all parts, laid end to end along the dimension named above; an argument that names none is the same for every part. Nothing has to cross between parts.
Inputs may be any that keep to these rules, and one draw needn't show every extreme that they name: `halo_source`: the value 2 * 128 means a zero halo cell and occurs on the lower side of the ocean tile of local index 0; the atmosphere tiles at both ends of their arc and the last ocean tile read their own edge row on their outer side. `dst_cells`: entry 2048 marks an unused block; a block is used only if its source tile lies in the other component, and every tile uses all 4 blocks of offset 0.
All inputs are finite; a program needn't handle non-finite values.
Results may differ from the reference program's by a relative error of at most 0.0085.
Values may be sent and summed in bfloat16 or wider, within the bound.
No kernel may reach another device: no remote copies, remote signals or barrier semaphores. Data moves between devices by JAX's collectives and lax.ppermute only.
A program may use at most 64 MiB of HBM per device.

```python
import jax
import jax.numpy as jnp
from jax import lax

C = 256
PROJ = 128
TH = 16
W = 128
BLOCK = 128
CAP = 4
REACH = 2
OFFSETS = 5
CELLS = 2048
TILE_COUNT = 16
HALF = 8


def draw_halo_source(key, part):
    tile = jnp.arange(TILE_COUNT, dtype=jnp.int32)[:, None, None]
    side = jnp.arange(2, dtype=jnp.int32)[None, :, None]
    column = jnp.arange(W, dtype=jnp.int32)[None, None, :]
    shift_amount = jax.random.randint(jax.random.fold_in(key, 11), (TILE_COUNT, 2, 1), 0, W)
    inner = (column + shift_amount) % W
    position = (tile + HALF // 2) % TILE_COUNT
    local = position % HALF
    ocean = position >= HALF
    polar = W + (column + W // 2) % W
    folded = W + (W - 1 - column)
    zeroed = jnp.zeros_like(inner) + 2 * W
    lower_end = (local == 0) & (side == 0)
    upper_end = (local == HALF - 1) & (side == 1)
    value = jnp.where(lower_end, jnp.where(ocean, zeroed, polar), jnp.where(upper_end, jnp.where(ocean, folded, polar), inner))
    return value.astype(jnp.int32)


def draw_dst_cells(key, part):
    tile = jnp.arange(TILE_COUNT, dtype=jnp.int32)[:, None, None, None]
    slot = jnp.arange(OFFSETS, dtype=jnp.int32)[None, :, None, None]
    entry = jnp.arange(CAP, dtype=jnp.int32)[None, None, :, None]
    position = (tile + HALF // 2) % TILE_COUNT
    local = position % HALF
    source_local = local - (slot - REACH)
    valid = (source_local >= 0) & (source_local < HALF)
    used_count = jax.random.randint(jax.random.fold_in(key, 21), (TILE_COUNT, OFFSETS, 1, 1), 1, CAP + 1)
    used_count = jnp.where(slot == REACH, CAP, used_count)
    used = valid & (entry < used_count)
    cell = jax.random.randint(jax.random.fold_in(key, 22), (TILE_COUNT, OFFSETS, CAP, BLOCK), 0, CELLS)
    return jnp.where(used, cell, CELLS).astype(jnp.int32)


def plant(array, rng, smallest, largest):
    index_at = [jax.random.randint(jax.random.fold_in(rng, axis), (), 0, length) for axis, length in enumerate(array.shape)]
    longest = array.shape.index(max(array.shape))
    next_to = index_at[:longest] + [(index_at[longest] + 1) % array.shape[longest]] + index_at[longest + 1:]
    return array.at[tuple(index_at)].set(smallest).at[tuple(next_to)].set(largest)


def levels(stream_key, dims, split, smallest, high):
    factor_of = 1.0
    for axis_at, blocks in split:
        heights = jax.random.uniform(jax.random.fold_in(jax.random.fold_in(stream_key, 6), axis_at), (blocks,), jnp.float32, smallest / len(split), high / len(split))
        factor_of = factor_of * jnp.repeat(jnp.exp(heights), dims[axis_at] // blocks).reshape((-1,) + (1,) * (len(dims) - 1 - axis_at))
    return factor_of


def noise(key, extent, spread, reach, shards=(), held_as=jnp.bfloat16):
    loudness = levels(key, extent, shards, -0.22, 0.18) if shards else 1.0
    entries = jax.random.normal(key, extent, jnp.float32) * spread * loudness
    return jnp.minimum(jnp.maximum(entries, -reach), reach).astype(held_as)


def setup_inputs(seed: int = 0, part: int = 0) -> dict:
    streams_of = jax.random.split(jax.random.key(seed), 9)
    part_splits = jax.random.split(jax.random.fold_in(streams_of[8], part), 9)
    return {
        "features": noise(part_splits[0], (TILE_COUNT, C, CELLS), 1.0, 6.0, ((0, 16),)),
        "conv_weight": noise(streams_of[1], (2, 2, 9, C, C), (9 * C) ** -0.5, 0.125),
        "proj_weight": noise(streams_of[2], (2, C, PROJ), C ** -0.5, 0.375),
        "back_weight": noise(streams_of[3], (2, PROJ, C), PROJ ** -0.5, 0.5),
        "sea_fraction": jnp.clip(1.0 * jax.random.uniform(streams_of[4], (TILE_COUNT, CELLS), jnp.float32) ** levels(streams_of[4], (TILE_COUNT, CELLS), ((0, 16),), -0.2, 0.2), 0.0, 1.0),
        "halo_source": draw_halo_source(jax.random.fold_in(streams_of[8], 71), part),
        "src_cells": plant(jax.random.randint(streams_of[6], (TILE_COUNT, OFFSETS, CAP, BLOCK), 0, CELLS), jax.random.fold_in(streams_of[6], 1), 0, CELLS - 1).astype(jnp.int32),
        "dst_cells": draw_dst_cells(jax.random.fold_in(streams_of[8], 71), part),
    }


def activate(values):
    return jax.nn.gelu(values.astype(jnp.float32), approximate=True).astype(jnp.bfloat16)


def convolve(kernel, padded):
    result = jnp.zeros((kernel.shape[2], TH, W), jnp.float32)
    for row_off in range(3):
        for col_off in range(3):
            shifted = jnp.roll(padded[:, row_off:row_off + TH, :], 1 - col_off, axis=2)
            result = result + jnp.einsum('io,irc->orc', kernel[row_off * 3 + col_off].astype(jnp.float32), shifted.astype(jnp.float32))
    return result


def residual_block(state, layer, conv_weight, component, wet_weight, halo_source):
    activated = activate(state).reshape(TILE_COUNT, C, TH, W)
    first_rows = activated[:, :, 0, :]
    last_rows = activated[:, :, TH - 1, :]
    from_below = jnp.roll(last_rows, 1, axis=0)
    from_above = jnp.roll(first_rows, -1, axis=0)
    zero_col = jnp.zeros((TILE_COUNT, C, 1), jnp.bfloat16)
    lower_src = jnp.concatenate([from_below, first_rows, zero_col], axis=2)
    upper_src = jnp.concatenate([from_above, last_rows, zero_col], axis=2)
    pick = jax.vmap(lambda source, index: jnp.take(source, index, axis=1))
    lower_row = pick(lower_src, halo_source[:, 0])
    upper_row = pick(upper_src, halo_source[:, 1])
    padded = jnp.concatenate([lower_row[:, :, None], activated, upper_row[:, :, None]], axis=2)

    def one_tile(inputs):
        pad_tile, comp_tile, state_tile, wet_tile = inputs
        kernel = conv_weight[comp_tile, layer]
        conv = convolve(kernel, pad_tile).reshape(C, CELLS)
        return (state_tile.astype(jnp.float32) + wet_tile[None, :] * conv).astype(jnp.bfloat16)

    return lax.map(one_tile, (padded, component, state, wet_weight))


def remap_add(state, component, proj_weight, back_weight, src_cells, dst_cells):
    def project(inputs):
        state_tile, comp_tile = inputs
        return jnp.einsum('cn,ck->nk', state_tile.astype(jnp.float32), proj_weight[comp_tile].astype(jnp.float32)).astype(jnp.bfloat16)

    projected = lax.map(project, (state, component))
    blocks = jax.vmap(lambda table, index: table[index])(projected, src_cells)
    incoming = jnp.stack([jnp.roll(blocks[:, slot], HALF + slot - REACH, axis=0) for slot in range(OFFSETS)], axis=1)

    def land(received, index):
        summed = jnp.zeros((CELLS, PROJ), jnp.float32)
        return summed.at[index.reshape(-1)].add(received.reshape(-1, PROJ).astype(jnp.float32), mode='drop')

    remapped = jax.vmap(land)(incoming, dst_cells).astype(jnp.bfloat16)

    def add_back(inputs):
        state_tile, remap_tile, comp_tile = inputs
        returned = jnp.einsum('nk,ko->on', remap_tile.astype(jnp.float32), back_weight[comp_tile].astype(jnp.float32))
        return (state_tile.astype(jnp.float32) + returned).astype(jnp.bfloat16)

    return lax.map(add_back, (state, remapped, component))


def reference(features, conv_weight, proj_weight, back_weight, sea_fraction, halo_source, src_cells, dst_cells):
    position = (jnp.arange(TILE_COUNT, dtype=jnp.int32) + HALF // 2) % TILE_COUNT
    component = (position >= HALF).astype(jnp.int32)
    wet_weight = jnp.where(component[:, None] == 1, sea_fraction, jnp.float32(1.0))
    state = residual_block(features, 0, conv_weight, component, wet_weight, halo_source)
    state = remap_add(state, component, proj_weight, back_weight, src_cells, dst_cells)
    state = residual_block(state, 1, conv_weight, component, wet_weight, halo_source)
    return state
```

```python
import functools

import jax
import jax.numpy as jnp
from jax import lax
from jax.experimental import pallas as pl
from jax.experimental.pallas import tpu as pltpu
from jax.sharding import PartitionSpec as P

F32 = jnp.float32
BF16 = jnp.bfloat16


def dot(a, b):
    return jnp.dot(a, b, preferred_element_type=F32)


def gelu(x):
    return jax.nn.gelu(x, approximate=True)


def column(row, width):
    return jnp.broadcast_to(row, (width, row.shape[1])).T


def wet_column(comp, sea_ref, start, size):
    row = jnp.where(comp == 1, sea_ref[:, start : start + size], F32(1.0))
    col = column(row, size)
    return col


def fill_shifted(xs_ref, row, act):
    width = act.shape[0]
    at = pl.ds(row * width, width)
    xs_ref[0, at, :] = pltpu.roll(act, 1, 0).astype(BF16)
    xs_ref[1, at, :] = act.astype(BF16)
    xs_ref[2, at, :] = pltpu.roll(act, width - 1, 0).astype(BF16)


def conv_rows(xs_ref, w_ref, first, rows, width):
    acc = None
    for a in range(3):
        for b in range(3):
            part = dot(xs_ref[b, pl.ds((first + a) * width, rows * width), :], w_ref[3 * a + b])
            acc = part if acc is None else acc + part
    return acc


def zero_halo(xs_ref, rows, width):
    zeros = jnp.zeros((3, width, xs_ref.shape[2]), BF16)
    xs_ref[:, pl.ds(0, width), :] = zeros
    xs_ref[:, pl.ds((rows + 1) * width, width), :] = zeros


def first_block_kernel(comp_ref, x_ref, w_ref, sea_ref, state_ref, part_ref, xs_ref, *, rows, width, group):
    comp = comp_ref[0]
    channels = x_ref.shape[0]
    zero_halo(xs_ref, rows, width)
    for r in range(rows):
        xt = x_ref[:, r * width : (r + 1) * width].astype(F32).T
        state_ref[pl.ds(r * width, width), :] = xt.astype(BF16)
        fill_shifted(xs_ref, r + 1, gelu(xt))
    for g in range(0, rows, group):
        acc = conv_rows(xs_ref, w_ref, g, group, width)
        for r in range(g, g + group):
            piece = acc[(r - g) * width : (r - g + 1) * width]
            if r == 0:
                part_ref[0] = piece
            elif r == rows - 1:
                part_ref[1] = piece
            else:
                wet = wet_column(comp, sea_ref, r * width, width)
                at = pl.ds(r * width, width)
                wide = jnp.concatenate([wet] * (channels // width), axis=1)
                state_ref[at, :] = (state_ref[at, :].astype(F32) + wide * piece).astype(BF16)


def second_block_kernel(comp_ref, s_ref, w_ref, sea_ref, out_ref, part_ref, xs_ref, *, rows, width, group):
    comp = comp_ref[0]
    channels = s_ref.shape[1]
    zero_halo(xs_ref, rows, width)
    for r in range(rows):
        fill_shifted(xs_ref, r + 1, gelu(s_ref[pl.ds(r * width, width), :].astype(F32)))
    for g in range(0, rows, group):
        acc = conv_rows(xs_ref, w_ref, g, group, width)
        for r in range(g, g + group):
            piece = acc[(r - g) * width : (r - g + 1) * width]
            if r == 0:
                part_ref[0] = piece
            elif r == rows - 1:
                part_ref[1] = piece
            else:
                row = jnp.where(comp == 1, sea_ref[:, r * width : (r + 1) * width], F32(1.0))
                state = s_ref[pl.ds(r * width, width), :].astype(F32).T
                out_ref[:, r * width : (r + 1) * width] = (state + row * piece.T).astype(BF16)


def pick_halo(index_row, received, own):
    width = index_row.shape[1]
    index = column(index_row.astype(F32), width)
    lane = lax.broadcasted_iota(jnp.int32, (width, width), 1).astype(F32)
    first = (index == lane).astype(F32).astype(BF16)
    second = (index == lane + width).astype(F32).astype(BF16)
    return dot(first, received) + dot(second, own)


def halo_conv(halo, w_ref, first_tap):
    width = halo.shape[0]
    return (
        dot(pltpu.roll(halo, 1, 0).astype(BF16), w_ref[first_tap])
        + dot(halo.astype(BF16), w_ref[first_tap + 1])
        + dot(pltpu.roll(halo, width - 1, 0).astype(BF16), w_ref[first_tap + 2])
    )


def project_kernel(
    comp_ref, s_ref, part_ref, lo_ref, hi_ref, table_ref, w_ref, sea_ref, p_ref, src_ref,
    edge_ref, out_ref, *, rows, width, groups,
):
    comp = comp_ref[0]
    channels = s_ref.shape[1]
    cells = rows * width
    coupling = p_ref.shape[1]
    weight = p_ref[...]
    edges = []
    for side in range(2):
        r = 0 if side == 0 else rows - 1
        received = gelu((lo_ref if side == 0 else hi_ref)[...].astype(F32).T).astype(BF16)
        own_state = s_ref[pl.ds(r * width, width), :].astype(F32)
        own = gelu(own_state).astype(BF16)
        halo = pick_halo(table_ref[side : side + 1, :], received, own)
        acc = part_ref[side] + halo_conv(halo, w_ref, 6 * side)
        wet = wet_column(comp, sea_ref, r * width, width)
        wide = jnp.concatenate([wet] * (channels // width), axis=1)
        edge = (own_state + wide * acc).astype(BF16)
        edge_ref[side] = edge
        edges.append(dot(edge, weight).astype(BF16))
    inner = dot(s_ref[pl.ds(width, cells - 2 * width), :], weight).astype(BF16)
    projected = jnp.concatenate([edges[0], inner, edges[1]], axis=0)
    depth = cells // groups
    wide = jnp.concatenate([projected[g * depth : (g + 1) * depth] for g in range(groups)], axis=1)
    lane = lax.broadcasted_iota(jnp.int32, (width, width), 1).astype(F32)
    tiles = depth // width
    for slot in range(out_ref.shape[0]):
        for block in range(out_ref.shape[1] // width):
            row = slot * (out_ref.shape[1] // width) + block
            index = column(src_ref[row : row + 1, :].astype(F32), width)
            group = jnp.floor(index * F32(1.0 / depth))
            inside = index - group * depth
            hot = jnp.concatenate(
                [(inside == lane + k * width).astype(F32).astype(BF16) for k in range(tiles)], axis=1
            )
            taken = dot(hot, wide)
            picked = taken[:, :coupling]
            for g in range(1, groups):
                picked = jnp.where(group == g, taken[:, g * coupling : (g + 1) * coupling], picked)
            out_ref[slot, block * width : (block + 1) * width, :] = picked.astype(BF16)


def land_kernel(comp_ref, *refs, rows, width, groups, slots):
    received = refs[:slots]
    dst_ref, s_ref, edge_ref, b_ref, state_ref, act_ref = refs[slots:]
    cells = rows * width
    coupling = b_ref.shape[0]
    depth = cells // groups
    per_slot = received[0].shape[0] // width
    sub = lax.broadcasted_iota(jnp.int32, (width, width), 0).astype(F32)
    total = None
    for slot in range(slots):
        sides, hots = [], []
        for block in range(per_slot):
            row = slot * per_slot + block
            index = dst_ref[row : row + 1, :].astype(F32)
            group = jnp.floor(index * F32(1.0 / depth))
            inside = index - group * depth
            values = received[slot][block * width : (block + 1) * width, :].astype(F32)
            group_col = column(group, width)
            sides.append(
                jnp.concatenate(
                    [jnp.where(group_col == g, values, 0.0).astype(BF16) for g in range(groups)], axis=1
                )
            )
            hots.append(
                jnp.concatenate(
                    [(inside == sub + k * width).astype(F32).astype(BF16) for k in range(depth // width)], axis=0
                )
            )
        part = dot(jnp.concatenate(hots, axis=1), jnp.concatenate(sides, axis=0))
        total = part if total is None else total + part
    for g in range(groups):
        remapped = total[:, g * coupling : (g + 1) * coupling].astype(BF16)
        returned = dot(remapped, b_ref[...])
        for k in range(depth // width):
            r = g * (depth // width) + k
            if r == 0:
                before = edge_ref[0]
            elif r == rows - 1:
                before = edge_ref[1]
            else:
                before = s_ref[pl.ds(r * width, width), :]
            state = (before.astype(F32) + returned[k * width : (k + 1) * width]).astype(BF16)
            state_ref[pl.ds(r * width, width), :] = state
            if r == 0:
                act_ref[0] = gelu(state.astype(F32)).astype(BF16)
            elif r == rows - 1:
                act_ref[1] = gelu(state.astype(F32)).astype(BF16)


def finish_kernel(comp_ref, out_in_ref, s_ref, part_ref, act_ref, lo_ref, hi_ref, table_ref, w_ref, sea_ref, out_ref):
    del out_in_ref
    comp = comp_ref[0]
    side = pl.program_id(0)

    def one(which, r_ref):
        halo = pick_halo(table_ref[which : which + 1, :], r_ref[...], act_ref[which])
        acc = part_ref[which] + halo_conv(halo, w_ref, 6 * which)
        row = jnp.where(comp == 1, sea_ref[...], F32(1.0))
        state = s_ref[...].astype(F32).T
        out_ref[...] = (state + row * acc.T).astype(BF16)

    pl.when(side == 0)(lambda: one(0, lo_ref))
    pl.when(side == 1)(lambda: one(1, hi_ref))


def whole(shape):
    return pl.BlockSpec(shape, lambda *_: (0,) * len(shape))


def call(kernel, comp, args, specs, out_shape, out_specs, scratch=(), grid=(1,), aliases=None, name=None):
    return pl.pallas_call(
        kernel,
        grid_spec=pltpu.PrefetchScalarGridSpec(
            num_scalar_prefetch=1, grid=grid, in_specs=specs, out_specs=out_specs, scratch_shapes=scratch
        ),
        out_shape=out_shape,
        input_output_aliases=aliases or {},
        name=name,
    )(comp, *args)


def on_device(
    features, conv_weight, proj_weight, back_weight, sea_fraction, halo_source, src_cells, dst_cells
):
    tile_total = lax.axis_size("tiles")
    half = tile_total // 2
    position = (lax.axis_index("tiles") + half // 2) % tile_total
    comp = (position >= half).astype(jnp.int32).reshape(1)
    _, channels, cells = features.shape
    width = halo_source.shape[-1]
    rows = cells // width
    coupling = proj_weight.shape[-1]
    slots = src_cells.shape[1]
    reach = slots // 2
    sent = src_cells.shape[2] * src_cells.shape[3]
    taps = conv_weight.shape[2]

    up = [(t, (t + 1) % tile_total) for t in range(tile_total)]
    down = [(b, a) for a, b in up]

    def remap_pairs(slot):
        pairs = []
        for t in range(tile_total):
            local = (t + half // 2) % tile_total % half
            d = slot - reach
            if 0 <= local - d < half:
                pairs.append(((t - half - d) % tile_total, t))
        return pairs

    def weight_spec(block):
        return pl.BlockSpec((None, None, taps, channels, channels), lambda i, c: (c[0], block, 0, 0, 0))

    def comp_spec(array):
        return pl.BlockSpec((None,) + array.shape[1:], lambda i, c: (c[0],) + (0,) * (array.ndim - 1))

    x = features[0]
    table = halo_source[0]
    src = src_cells[0].reshape(-1, width)
    dst = dst_cells[0].reshape(-1, width)

    lo = lax.ppermute(x[:, cells - width :], "tiles", up)
    hi = lax.ppermute(x[:, :width], "tiles", down)

    part_shape = jax.ShapeDtypeStruct((2, width, channels), F32)
    edge_shape = jax.ShapeDtypeStruct((2, width, channels), BF16)
    state_shape = jax.ShapeDtypeStruct((cells, channels), BF16)
    shifted = pltpu.VMEM((3, (rows + 2) * width, channels), BF16)
    group = 4

    state, part = call(
        functools.partial(first_block_kernel, rows=rows, width=width, group=group),
        comp,
        (x, conv_weight, sea_fraction),
        [whole(x.shape), weight_spec(0), whole(sea_fraction.shape)],
        (state_shape, part_shape),
        (whole(state_shape.shape), whole(part_shape.shape)),
        scratch=[shifted],
        name="block0",
    )
    edge, outgoing = call(
        functools.partial(project_kernel, rows=rows, width=width, groups=4),
        comp,
        (state, part, lo, hi, table, conv_weight, sea_fraction, proj_weight, src),
        [
            whole(state.shape), whole(part.shape), whole(lo.shape), whole(hi.shape), whole(table.shape),
            weight_spec(0), whole(sea_fraction.shape), comp_spec(proj_weight), whole(src.shape),
        ],
        (edge_shape, jax.ShapeDtypeStruct((slots, sent, coupling), BF16)),
        (whole(edge_shape.shape), whole((slots, sent, coupling))),
        name="project",
    )
    received = [lax.ppermute(outgoing[s], "tiles", remap_pairs(s)) for s in range(slots)]
    state, act = call(
        functools.partial(land_kernel, rows=rows, width=width, groups=2, slots=slots),
        comp,
        (*received, dst, state, edge, back_weight),
        [whole(r.shape) for r in received]
        + [whole(dst.shape), whole(state.shape), whole(edge.shape), comp_spec(back_weight)],
        (state_shape, edge_shape),
        (whole(state_shape.shape), whole(edge_shape.shape)),
        name="land",
    )
    lo = lax.ppermute(act[1], "tiles", up)
    hi = lax.ppermute(act[0], "tiles", down)
    out, part = call(
        functools.partial(second_block_kernel, rows=rows, width=width, group=group),
        comp,
        (state, conv_weight, sea_fraction),
        [whole(state.shape), weight_spec(1), whole(sea_fraction.shape)],
        (jax.ShapeDtypeStruct((channels, cells), BF16), part_shape),
        (whole((channels, cells)), whole(part_shape.shape)),
        scratch=[shifted],
        name="block1",
    )
    out = call(
        finish_kernel,
        comp,
        (out, state, part, act, lo, hi, table, conv_weight, sea_fraction),
        [
            pl.BlockSpec(memory_space=pl.ANY),
            pl.BlockSpec((width, channels), lambda i, c: (i * (rows - 1), 0)),
            whole(part.shape), whole(act.shape), whole(lo.shape), whole(hi.shape), whole(table.shape),
            weight_spec(1),
            pl.BlockSpec((1, width), lambda i, c: (0, i * (rows - 1))),
        ],
        jax.ShapeDtypeStruct((channels, cells), BF16),
        pl.BlockSpec((channels, width), lambda i, c: (0, i * (rows - 1))),
        grid=(2,),
        aliases={1: 0},
        name="finish",
    )
    return out[None]


def solution(mesh):
    placed = (
        P(("runs", "tiles"), None, None),
        P(),
        P(),
        P(),
        P("tiles", None),
        P("tiles", None, None),
        P("tiles", None, None, None),
        P("tiles", None, None, None),
    )
    return jax.shard_map(
        on_device,
        mesh=mesh,
        in_specs=placed,
        out_specs=P(("runs", "tiles"), None, None),
        check_vma=False,
    )
```

```python
import functools

import jax
import jax.numpy as jnp
from jax import lax
from jax.experimental import pallas as pl
from jax.experimental.pallas import tpu as pltpu
from jax.sharding import PartitionSpec as P

F32 = jnp.float32
BF16 = jnp.bfloat16


def dot(a, b):
    return jnp.dot(a, b, preferred_element_type=F32)


def gelu(x):
    return jax.nn.gelu(x, approximate=True)


def column(row, width):
    return jnp.broadcast_to(row, (width, row.shape[1])).T


def wet_column(comp, sea_ref, start, size):
    row = jnp.where(comp == 1, sea_ref[:, start : start + size], F32(1.0))
    col = column(row, size)
    return col


def fill_shifted(xs_ref, row, act):
    width = act.shape[0]
    at = pl.ds(row * width, width)
    xs_ref[0, at, :] = pltpu.roll(act, 1, 0).astype(BF16)
    xs_ref[1, at, :] = act.astype(BF16)
    xs_ref[2, at, :] = pltpu.roll(act, width - 1, 0).astype(BF16)


def conv_rows(xs_ref, w_ref, first, rows, width):
    acc = None
    for a in range(3):
        for b in range(3):
            part = dot(xs_ref[b, pl.ds((first + a) * width, rows * width), :], w_ref[3 * a + b])
            acc = part if acc is None else acc + part
    return acc


def zero_halo(xs_ref, rows, width):
    zeros = jnp.zeros((3, width, xs_ref.shape[2]), BF16)
    xs_ref[:, pl.ds(0, width), :] = zeros
    xs_ref[:, pl.ds((rows + 1) * width, width), :] = zeros


def wide_column(comp, sea_ref, start, size, channels):
    return jnp.concatenate([wet_column(comp, sea_ref, start, size)] * (channels // size), axis=1)


def first_block_kernel(
    comp_ref, x_ref, sea_ref, conv_hbm, state_ref, part_ref, w0_ref, w1_ref, xs_ref, sems, *, rows, width, group
):
    comp = comp_ref[0]
    channels = x_ref.shape[0]
    taps = w0_ref.shape[0]
    early = [
        pltpu.make_async_copy(conv_hbm.at[comp, 0, pl.ds(k, 1)], w0_ref.at[pl.ds(k, 1)], sems.at[k])
        for k in range(taps)
    ]
    late = pltpu.make_async_copy(conv_hbm.at[comp, 1], w1_ref, sems.at[taps])
    for copy in early:
        copy.start()
    late.start()
    zero_halo(xs_ref, rows, width)
    for r in range(rows):
        xt = x_ref[:, r * width : (r + 1) * width].astype(F32).T
        state_ref[pl.ds(r * width, width), :] = xt.astype(BF16)
        fill_shifted(xs_ref, r + 1, gelu(xt))
    for copy in early:
        copy.wait()
    for g in range(0, rows, group):
        acc = conv_rows(xs_ref, w0_ref, g, group, width)
        for r in range(g, g + group):
            piece = acc[(r - g) * width : (r - g + 1) * width]
            if r == 0:
                part_ref[0] = piece
            elif r == rows - 1:
                part_ref[1] = piece
            else:
                at = pl.ds(r * width, width)
                wet = wide_column(comp, sea_ref, r * width, width, channels)
                state_ref[at, :] = (state_ref[at, :].astype(F32) + wet * piece).astype(BF16)
    late.wait()


def pick_halo(index_row, received, own):
    width = index_row.shape[1]
    index = column(index_row.astype(F32), width)
    lane = lax.broadcasted_iota(jnp.int32, (width, width), 1).astype(F32)
    first = (index == lane).astype(F32).astype(BF16)
    second = (index == lane + width).astype(F32).astype(BF16)
    return dot(first, received) + dot(second, own)


def halo_conv(halo, w_ref, first_tap):
    width = halo.shape[0]
    return (
        dot(pltpu.roll(halo, 1, 0).astype(BF16), w_ref[first_tap])
        + dot(halo.astype(BF16), w_ref[first_tap + 1])
        + dot(pltpu.roll(halo, width - 1, 0).astype(BF16), w_ref[first_tap + 2])
    )


def gather_rows(wide, index_rows, groups):
    width = index_rows.shape[1]
    depth = wide.shape[0]
    coupling = wide.shape[1] // groups
    lane = lax.broadcasted_iota(jnp.int32, (width, width), 1).astype(F32)
    hots, picks = [], []
    for block in range(index_rows.shape[0]):
        index = column(index_rows[block : block + 1, :].astype(F32), width)
        group = jnp.floor(index * F32(1.0 / depth))
        inside = index - group * depth
        hots.append(
            jnp.concatenate(
                [(inside == lane + k * width).astype(F32).astype(BF16) for k in range(depth // width)], axis=1
            )
        )
        picks.append(group)
    taken = dot(jnp.concatenate(hots, axis=0), wide)
    group = jnp.concatenate(picks, axis=0)
    picked = taken[:, :coupling]
    for g in range(1, groups):
        picked = jnp.where(group == g, taken[:, g * coupling : (g + 1) * coupling], picked)
    return picked.astype(BF16)


def project_kernel(
    comp_ref, s_ref, part_ref, lo_ref, hi_ref, table_ref, w_ref, sea_ref, p_ref, src_ref,
    edge_ref, wide_ref, out_ref, *, rows, width, groups, slot,
):
    comp = comp_ref[0]
    channels = s_ref.shape[1]
    cells = rows * width
    weight = p_ref[comp]
    edges = []
    for side in range(2):
        r = 0 if side == 0 else rows - 1
        received = gelu((lo_ref if side == 0 else hi_ref)[...].astype(F32).T).astype(BF16)
        own_state = s_ref[pl.ds(r * width, width), :].astype(F32)
        own = gelu(own_state).astype(BF16)
        halo = pick_halo(table_ref[side : side + 1, :], received, own)
        acc = part_ref[side] + halo_conv(halo, w_ref, 6 * side)
        edge = (own_state + wide_column(comp, sea_ref, r * width, width, channels) * acc).astype(BF16)
        edge_ref[side] = edge
        edges.append(dot(edge, weight).astype(BF16))
    inner = dot(s_ref[pl.ds(width, cells - 2 * width), :], weight).astype(BF16)
    projected = jnp.concatenate([edges[0], inner, edges[1]], axis=0)
    depth = cells // groups
    wide_ref[...] = jnp.concatenate([projected[g * depth : (g + 1) * depth] for g in range(groups)], axis=1)
    out_ref[...] = gather_rows(wide_ref[...], src_ref[slot], groups)


def gather_kernel(wide_ref, src_ref, *out_refs, groups, slots):
    for slot, out_ref in zip(slots, out_refs):
        out_ref[...] = gather_rows(wide_ref[...], src_ref[slot], groups)


def land_rows(received, index_rows, depth, groups):
    width = index_rows.shape[1]
    sub = lax.broadcasted_iota(jnp.int32, (width, width), 0).astype(F32)
    sides, hots = [], []
    for block in range(index_rows.shape[0]):
        index = index_rows[block : block + 1, :].astype(F32)
        group = jnp.floor(index * F32(1.0 / depth))
        inside = index - group * depth
        values = received[block * width : (block + 1) * width, :].astype(F32)
        group_col = column(group, width)
        sides.append(
            jnp.concatenate([jnp.where(group_col == g, values, 0.0).astype(BF16) for g in range(groups)], axis=1)
        )
        hots.append(
            jnp.concatenate(
                [(inside == sub + k * width).astype(F32).astype(BF16) for k in range(depth // width)], axis=0
            )
        )
    return dot(jnp.concatenate(hots, axis=1), jnp.concatenate(sides, axis=0))


def land_first_kernel(recv_ref, dst_ref, total_ref, *, slot, groups):
    total_ref[...] = land_rows(recv_ref[...], dst_ref[slot], total_ref.shape[0], groups)


def land_more_kernel(recv_ref, dst_ref, before_ref, total_ref, *, slot, groups):
    total_ref[...] = before_ref[...] + land_rows(recv_ref[...], dst_ref[slot], total_ref.shape[0], groups)


def land_last_kernel(
    comp_ref, recv_ref, dst_ref, before_ref, s_ref, edge_ref, b_ref, state_ref, first_ref, last_ref,
    *, rows, width, groups, slot,
):
    depth = before_ref.shape[0]
    weight = b_ref[comp_ref[0]]
    coupling = weight.shape[0]
    total = before_ref[...] + land_rows(recv_ref[...], dst_ref[slot], depth, groups)
    for g in range(groups):
        remapped = total[:, g * coupling : (g + 1) * coupling].astype(BF16)
        returned = dot(remapped, weight)
        for k in range(depth // width):
            r = g * (depth // width) + k
            if r == 0:
                before = edge_ref[0]
            elif r == rows - 1:
                before = edge_ref[1]
            else:
                before = s_ref[pl.ds(r * width, width), :]
            state = (before.astype(F32) + returned[k * width : (k + 1) * width]).astype(BF16)
            state_ref[pl.ds(r * width, width), :] = state
            if r == 0:
                first_ref[...] = gelu(state.astype(F32)).astype(BF16)
            elif r == rows - 1:
                last_ref[...] = gelu(state.astype(F32)).astype(BF16)


def second_block_kernel(
    comp_ref, s_ref, w_ref, sea_ref, out_hbm, part_ref, xs_ref, out_ref, sems, *, rows, width, group
):
    comp = comp_ref[0]
    zero_halo(xs_ref, rows, width)
    for r in range(rows):
        fill_shifted(xs_ref, r + 1, gelu(s_ref[pl.ds(r * width, width), :].astype(F32)))
    copies = []
    for g in range(0, rows, group):
        acc = conv_rows(xs_ref, w_ref, g, group, width)
        for r in range(g, g + group):
            piece = acc[(r - g) * width : (r - g + 1) * width]
            if r == 0:
                part_ref[0] = piece
            elif r == rows - 1:
                part_ref[1] = piece
            else:
                row = jnp.where(comp == 1, sea_ref[:, r * width : (r + 1) * width], F32(1.0))
                state = s_ref[pl.ds(r * width, width), :].astype(F32).T
                out_ref[:, r * width : (r + 1) * width] = (state + row * piece.T).astype(BF16)
        lo = max(g, 1) * width
        at = pl.ds(lo, min(g + group, rows - 1) * width - lo)
        copy = pltpu.make_async_copy(out_ref.at[:, at], out_hbm.at[:, at], sems.at[g // group])
        copy.start()
        copies.append(copy)
    for copy in copies:
        copy.wait()


def finish_kernel(
    comp_ref, out_in, s_ref, part_ref, first_ref, last_ref, lo_ref, hi_ref, table_ref, w_ref, sea_ref,
    out_hbm, buf_ref, sems, *, rows, width,
):
    del out_in
    comp = comp_ref[0]
    copies = []
    for side in range(2):
        r = 0 if side == 0 else rows - 1
        received = (lo_ref if side == 0 else hi_ref)[...]
        own = (first_ref if side == 0 else last_ref)[...]
        halo = pick_halo(table_ref[side : side + 1, :], received, own)
        acc = part_ref[side] + halo_conv(halo, w_ref, 6 * side)
        row = jnp.where(comp == 1, sea_ref[:, r * width : (r + 1) * width], F32(1.0))
        state = s_ref[pl.ds(r * width, width), :].astype(F32).T
        buf_ref[side] = (state + row * acc.T).astype(BF16)
        copy = pltpu.make_async_copy(buf_ref.at[side], out_hbm.at[:, pl.ds(r * width, width)], sems.at[side])
        copy.start()
        copies.append(copy)
    for copy in copies:
        copy.wait()


VMEM = pl.BlockSpec(memory_space=pltpu.VMEM)
SMEM = pl.BlockSpec(memory_space=pltpu.SMEM)
HBM = pl.BlockSpec(memory_space=pl.ANY)
GRANT = 24 << 20


def call(kernel, args, specs, out_shape, out_specs=None, scratch=(), aliases=None, name=None):
    placed = [pltpu.with_memory_space_constraint(a, pltpu.VMEM) if s is VMEM else a for a, s in zip(args, specs)]
    return pl.pallas_call(
        kernel,
        in_specs=specs,
        out_specs=out_specs or [VMEM] * len(out_shape),
        out_shape=out_shape,
        scratch_shapes=scratch,
        input_output_aliases=aliases or {},
        compiler_params=pltpu.CompilerParams(vmem_limit_bytes=GRANT),
        name=name,
    )(*placed)


def on_device(
    features, conv_weight, proj_weight, back_weight, sea_fraction, halo_source, src_cells, dst_cells
):
    tile_total = lax.axis_size("tiles")
    half = tile_total // 2
    position = (lax.axis_index("tiles") + half // 2) % tile_total
    comp = (position >= half).astype(jnp.int32).reshape(1)
    _, channels, cells = features.shape
    width = halo_source.shape[-1]
    rows = cells // width
    coupling = proj_weight.shape[-1]
    slots = src_cells.shape[1]
    reach = slots // 2
    sent = src_cells.shape[2] * src_cells.shape[3]
    taps = conv_weight.shape[2]
    group, gathered, landed = 4, 4, 2

    up = [(t, (t + 1) % tile_total) for t in range(tile_total)]
    down = [(b, a) for a, b in up]

    def remap_pairs(slot):
        d = slot - reach
        pairs = [
            ((t - half - d) % tile_total, t)
            for t in range(tile_total)
            if 0 <= (t + half // 2) % tile_total % half - d < half
        ]
        idle_sources = sorted(set(range(tile_total)) - {a for a, _ in pairs})
        idle_targets = sorted(set(range(tile_total)) - {b for _, b in pairs})
        return pairs + list(zip(idle_sources, idle_targets))

    x = features[0]
    table = halo_source[0]
    src = src_cells[0]
    dst = dst_cells[0]

    lo = lax.ppermute(x[:, cells - width :], "tiles", up)
    hi = lax.ppermute(x[:, :width], "tiles", down)

    state_shape = pltpu.VMEM((cells, channels), BF16)
    part_shape = pltpu.VMEM((2, width, channels), F32)
    edge_shape = pltpu.VMEM((2, width, channels), BF16)
    row_shape = pltpu.VMEM((width, channels), BF16)
    weight_shape = pltpu.VMEM((taps, channels, channels), BF16)
    sent_shape = pltpu.VMEM((sent, coupling), BF16)
    total_shape = pltpu.VMEM((cells // landed, landed * coupling), F32)
    shifted = pltpu.VMEM((3, (rows + 2) * width, channels), BF16)

    state, part, w0, w1 = call(
        functools.partial(first_block_kernel, rows=rows, width=width, group=group),
        (comp, x, sea_fraction, conv_weight),
        [SMEM, VMEM, VMEM, HBM],
        [state_shape, part_shape, weight_shape, weight_shape],
        scratch=[shifted, pltpu.SemaphoreType.DMA((taps + 1,))],
        name="block0",
    )
    order = [reach] + [s for s in range(slots) if s != reach]
    edge, wide, middle = call(
        functools.partial(project_kernel, rows=rows, width=width, groups=gathered, slot=order[0]),
        (comp, state, part, lo, hi, table, w0, sea_fraction, proj_weight, src),
        [SMEM] + [VMEM] * 9,
        [edge_shape, pltpu.VMEM((cells // gathered, gathered * coupling), BF16), sent_shape],
        name="project",
    )
    others = call(
        functools.partial(gather_kernel, groups=gathered, slots=order[1:]),
        (wide, src),
        [VMEM] * 2,
        [sent_shape] * (slots - 1),
        name="gather",
    )
    received = [lax.ppermute(o, "tiles", remap_pairs(s)) for s, o in zip(order, [middle, *others])]
    (total,) = call(
        functools.partial(land_first_kernel, slot=order[0], groups=landed),
        (received[0], dst), [VMEM] * 2, [total_shape], name="land_first",
    )
    for k in range(1, slots - 1):
        (total,) = call(
            functools.partial(land_more_kernel, slot=order[k], groups=landed),
            (received[k], dst, total), [VMEM] * 3, [total_shape], aliases={2: 0}, name="land_more",
        )
    state, first, last = call(
        functools.partial(land_last_kernel, rows=rows, width=width, groups=landed, slot=order[-1]),
        (comp, received[-1], dst, total, state, edge, back_weight),
        [SMEM] + [VMEM] * 6,
        [state_shape, row_shape, row_shape],
        name="land_last",
    )
    lo = lax.ppermute(last, "tiles", up)
    hi = lax.ppermute(first, "tiles", down)
    out_shape = jax.ShapeDtypeStruct((channels, cells), BF16)
    out, part = call(
        functools.partial(second_block_kernel, rows=rows, width=width, group=group),
        (comp, state, w1, sea_fraction),
        [SMEM] + [VMEM] * 3,
        [out_shape, part_shape],
        out_specs=[HBM, VMEM],
        scratch=[shifted, pltpu.VMEM((channels, cells), BF16), pltpu.SemaphoreType.DMA((rows // group,))],
        name="block1",
    )
    (out,) = call(
        functools.partial(finish_kernel, rows=rows, width=width),
        (comp, out, state, part, first, last, lo, hi, table, w1, sea_fraction),
        [SMEM, HBM] + [VMEM] * 9,
        [out_shape],
        out_specs=[HBM],
        scratch=[pltpu.VMEM((2, channels, width), BF16), pltpu.SemaphoreType.DMA((2,))],
        aliases={1: 0},
        name="finish",
    )
    return out[None]


def solution(mesh):
    placed = (
        P(("runs", "tiles"), None, None),
        P(),
        P(),
        P(),
        P("tiles", None),
        P("tiles", None, None),
        P("tiles", None, None, None),
        P("tiles", None, None, None),
    )
    return jax.shard_map(
        on_device,
        mesh=mesh,
        in_specs=placed,
        out_specs=P(("runs", "tiles"), None, None),
        check_vma=False,
    )
```
